32 devices in a mesh: shard: 8 (over z, y), tensor: 4 (over x, core).
Axes of the slice: x: 2, y: 2, z: 4, core: 2. Of those that a mesh axis runs over, the one named last changes fastest.
Arguments:
- acts: bfloat16 [2048, 1152], P('shard', 'tensor'), may hold values from -600 to 600
- outgrads: bfloat16 [2048, 1152], P('shard', 'tensor'), may hold values from -800 to 800
- weight: bfloat16 [1152, 1152], P('shard', 'tensor'), may hold values from -6 to 6
- momentum: float32 [1152, 1152], P('shard', 'tensor'), may hold values from -6 to 6
- damping: float32 [2], replicated, may hold values from 0.3 to 3
- coeffs: float32 [4], replicated, may hold values from 0.5 to 2
Outputs:
- new_momentum: float32 [1152, 1152], P('shard', 'tensor')
- gathered_weight: bfloat16 [1152, 1152], P(None, 'tensor')
The draws below stay inside these ranges and needn't reach their ends.
All inputs are finite; a program needn't handle non-finite values.
Results may differ from the reference program's by a relative error of at most 0.003.
The reference program's roundings to bfloat16 on the way (of `act_factor`, `grad_factor`, `grad_inverse` and `projected`) count: a program that leaves them out, or rounds other values in their place, can miss the bound.
Values may be sent and summed in bfloat16 or wider, within the bound.
A program may use at most 64 MiB of HBM per device.

```python
import math
import jax
import jax.numpy as jnp
from jax import lax

D = 1152
TERMS = 4
TOKENS = 2048


def draw_pair(key):
    base_key = jax.random.fold_in(key, 11)
    keys = jax.random.split(base_key, 4)
    col_pos = jnp.arange(D, dtype=jnp.float32)[None, :] / (D - 1)
    tok_pos = jnp.arange(TOKENS, dtype=jnp.float32)[:, None] / (TOKENS - 1)
    noise_act = jax.random.truncated_normal(keys[0], -4.0, 4.0, (TOKENS, D), jnp.float32)
    noise_grad = jax.random.truncated_normal(keys[1], -4.0, 4.0, (TOKENS, D), jnp.float32)
    col_scale = jnp.power(3.0, col_pos) * jnp.exp(jax.random.uniform(keys[2], (1, D), jnp.float32, 0.0, 1.2))
    row_scale = jnp.power(3.0, tok_pos) * jnp.exp(jax.random.uniform(keys[3], (TOKENS, 1), jnp.float32, 0.0, 1.0))
    mixed = noise_act + 0.5 * jnp.roll(noise_act, 1, axis=1)
    acts_value = mixed * col_scale * row_scale
    grad_mixed = 0.6 * jnp.roll(mixed, 5, axis=1) + noise_grad + 0.4 * jnp.roll(noise_grad, 3, axis=1)
    grads_value = grad_mixed * jnp.roll(col_scale, 5, axis=1) * row_scale
    return (acts_value, grads_value)


def draw_acts(key, part):
    return draw_pair(key)[0].astype(jnp.bfloat16)


def draw_outgrads(key, part):
    return draw_pair(key)[1].astype(jnp.bfloat16)


def steps_of(stream_key, shape, cuts, smallest, high):
    def one(dim, parts):
        heights = jax.random.uniform(jax.random.fold_in(jax.random.fold_in(stream_key, 6), dim), (parts,), jnp.float32, smallest / len(cuts), high / len(cuts))
        return jnp.repeat(jnp.exp(heights), shape[dim] // parts).reshape((-1,) + (1,) * (len(shape) - dim - 1))

    gain = one(*cuts[0])
    for cut in cuts[1:]:
        gain = gain * one(*cut)
    return gain


def centred(key, shape, width, reach, cuts=(), held_as=jnp.bfloat16):
    array = jax.random.normal(key, shape, jnp.float32) * width
    if len(cuts) > 0:
        array = steps_of(key, shape, cuts, -0.22, 0.18) * array
    return jnp.clip(array, min=-reach, max=reach).astype(held_as)


def setup_inputs(seed: int = 0) -> dict:
    key_of = jax.random.split(jax.random.key(seed), 7)
    acts = draw_acts(jax.random.fold_in(key_of[6], 71), 0)
    outgrads = draw_outgrads(jax.random.fold_in(key_of[6], 71), 0)
    weight = centred(key_of[2], (D, D), 1.0, 6.0, ((0, 8), (1, 4)))
    momentum = centred(key_of[3], (D, D), 1.0, 6.0, ((0, 8), (1, 4)), jnp.float32)
    damping = jnp.clip(jnp.exp(jax.random.uniform(key_of[4], (2,), jnp.float32, math.log(0.3), math.log(3.0))), 0.3, 3.0)
    coeffs = jnp.clip(jnp.exp(jax.random.uniform(key_of[5], (TERMS,), jnp.float32, math.log(0.5), math.log(2.0))), 0.5, 2.0)
    return {"acts": acts, "outgrads": outgrads, "weight": weight, "momentum": momentum, "damping": damping, "coeffs": coeffs}


def horner_columns(factor, coeffs, first_col, col_count, bound_norm):
    extent = factor.shape[0]
    row_ids = lax.broadcasted_iota(jnp.int32, (extent, col_count), 0)
    col_ids = lax.broadcasted_iota(jnp.int32, (extent, col_count), 1) + first_col
    identity_cols = (row_ids == col_ids).astype(jnp.float32)
    term_count = coeffs.shape[0]
    iterate = coeffs[term_count - 1] * identity_cols
    for term_index in range(term_count - 2, -1, -1):
        product = jnp.dot(factor, iterate.astype(jnp.bfloat16), preferred_element_type=jnp.float32)
        iterate = coeffs[term_index] * identity_cols + iterate - product / bound_norm
    return iterate

def reference(acts, outgrads, weight, momentum, damping, coeffs):
    act_cov = jnp.dot(acts.T, acts, preferred_element_type=jnp.float32)
    grad_cov = jnp.dot(outgrads.T, outgrads, preferred_element_type=jnp.float32)
    act_trace = jnp.sum(jnp.square(acts.astype(jnp.float32)))
    grad_trace = jnp.sum(jnp.square(outgrads.astype(jnp.float32)))
    identity = jnp.eye(D, dtype=jnp.float32)
    act_factor = (act_cov + damping[0] * act_trace / D * identity).astype(jnp.bfloat16)
    grad_factor = (grad_cov + damping[1] * grad_trace / D * identity).astype(jnp.bfloat16)
    act_scale = jnp.sqrt(jnp.sum(jnp.square(act_factor.astype(jnp.float32))))
    grad_scale = jnp.sqrt(jnp.sum(jnp.square(grad_factor.astype(jnp.float32))))
    act_inverse = horner_columns(act_factor, coeffs, 0, D, act_scale)
    grad_inverse = horner_columns(grad_factor, coeffs, 0, D, grad_scale).astype(jnp.bfloat16)
    projected = jnp.dot(outgrads, grad_inverse, preferred_element_type=jnp.float32).astype(jnp.bfloat16)
    right_product = jnp.dot(acts.T, projected, preferred_element_type=jnp.float32)
    update = jnp.dot(act_inverse.T, right_product, precision=lax.Precision.HIGHEST)
    mean_square = jnp.sum(update * update) / (D * D)
    new_momentum = 0.9 * momentum + update / jnp.sqrt(mean_square + 1e-06)
    gathered_weight = (weight.astype(jnp.float32) - 0.1 * new_momentum).astype(jnp.bfloat16)
    return (new_momentum, gathered_weight)
```

```python
import functools

import jax
import jax.numpy as jnp
from jax import lax
from jax.experimental import pallas as pl
from jax.experimental.pallas import tpu as pltpu
from jax.sharding import PartitionSpec as P

D = 1152


def horner_columns(factor, coeffs, first_col, col_count, bound_norm):
    extent = factor.shape[0]
    row_ids = lax.broadcasted_iota(jnp.int32, (extent, col_count), 0)
    col_ids = lax.broadcasted_iota(jnp.int32, (extent, col_count), 1) + first_col
    identity_cols = (row_ids == col_ids).astype(jnp.float32)
    term_count = coeffs.shape[0]
    iterate = coeffs[term_count - 1] * identity_cols
    for term_index in range(term_count - 2, -1, -1):
        product = jnp.dot(factor, iterate.astype(jnp.bfloat16), preferred_element_type=jnp.float32)
        iterate = coeffs[term_index] * identity_cols + iterate - product / bound_norm
    return iterate


def tokens_product(left, right):
    return lax.dot_general(
        left, right, (((0,), (0,)), ((), ())), preferred_element_type=jnp.float32
    )


def on_device(acts, outgrads, weight, momentum, damping, coeffs):
    row_count = weight.shape[0]
    col_count = weight.shape[1]
    row_first = lax.axis_index("shard") * row_count
    col_first = lax.axis_index("tensor") * col_count
    full_acts, full_grads = (
        lax.all_gather(acts, "tensor", axis=1, tiled=True),
        lax.all_gather(outgrads, "tensor", axis=1, tiled=True),
    )
    local_squares = jnp.stack(
        [
            jnp.sum(jnp.square(acts.astype(jnp.float32))),
            jnp.sum(jnp.square(outgrads.astype(jnp.float32))),
        ]
    )
    traces = lax.psum(local_squares, ("shard", "tensor"))
    act_part = tokens_product(full_acts, acts)
    grad_part = tokens_product(full_grads, outgrads)
    stats = lax.psum_scatter(
        jnp.concatenate([act_part, grad_part], axis=1), "shard", scatter_dimension=0, tiled=True
    )
    row_ids = lax.broadcasted_iota(jnp.int32, (row_count, col_count), 0) + row_first
    col_ids = lax.broadcasted_iota(jnp.int32, (row_count, col_count), 1) + col_first
    diag_mask = (row_ids == col_ids).astype(jnp.float32)
    act_piece = (stats[:, :col_count] + damping[0] * traces[0] / D * diag_mask).astype(jnp.bfloat16)
    grad_piece = (stats[:, col_count:] + damping[1] * traces[1] / D * diag_mask).astype(
        jnp.bfloat16
    )
    act_wide, grad_wide = (
        lax.all_gather(act_piece, "tensor", axis=1, tiled=True),
        lax.all_gather(grad_piece, "tensor", axis=1, tiled=True),
    )
    act_full, grad_full = (
        lax.all_gather(act_wide, "shard", axis=0, tiled=True),
        lax.all_gather(grad_wide, "shard", axis=0, tiled=True),
    )
    act_scale = jnp.sqrt(jnp.sum(jnp.square(act_full.astype(jnp.float32))))
    grad_scale = jnp.sqrt(jnp.sum(jnp.square(grad_full.astype(jnp.float32))))
    act_inverse = horner_columns(act_full, coeffs, row_first, row_count, act_scale)
    grad_inverse = horner_columns(grad_full, coeffs, col_first, col_count, grad_scale).astype(
        jnp.bfloat16
    )
    projected = jnp.dot(full_grads, grad_inverse, preferred_element_type=jnp.float32).astype(
        jnp.bfloat16
    )
    right_term = tokens_product(full_acts, projected)
    right_product = lax.psum(right_term, "shard")
    update = lax.dot_general(
        act_inverse,
        right_product,
        (((0,), (0,)), ((), ())),
        precision=lax.Precision.HIGHEST,
        preferred_element_type=jnp.float32,
    )
    square_sum = lax.psum(jnp.sum(update * update), ("shard", "tensor"))
    mean_square = square_sum / (D * D)
    new_momentum = 0.9 * momentum + update / jnp.sqrt(mean_square + 1e-06)
    new_weight = (weight.astype(jnp.float32) - 0.1 * new_momentum).astype(jnp.bfloat16)
    gathered_weight = lax.all_gather(new_weight, "shard", axis=0, tiled=True)
    return (new_momentum, gathered_weight)


MESH = pl.DeviceIdType.MESH
BF16 = jnp.bfloat16
F32 = jnp.float32
Y_CHIPS = 2
CORES = 2
TILES = 3


def dot_nt(left, right):
    return lax.dot_general(
        left, right, (((1,), (1,)), ((), ())), preferred_element_type=jnp.float32
    )


def dot_nn(left, right, precision=None):
    return lax.dot_general(
        left,
        right,
        (((1,), (0,)), ((), ())),
        precision=precision,
        preferred_element_type=jnp.float32,
    )


def eye(rows, cols, row_first, col_first):
    row_ids = lax.broadcasted_iota(jnp.int32, (rows, cols), 0) + row_first
    col_ids = lax.broadcasted_iota(jnp.int32, (rows, cols), 1) + col_first
    return row_ids == col_ids


def total(value):
    return jnp.sum(jnp.sum(value, axis=0, keepdims=True), axis=1, keepdims=True)


class Place:
    def __init__(self, shards):
        self.depth = shards // Y_CHIPS
        self.s = lax.axis_index("shard")
        self.t = lax.axis_index("tensor")
        self.z, self.y = self.s // Y_CHIPS, self.s % Y_CHIPS
        self.x, self.c = self.t // CORES, self.t % CORES
        c = self.c
        self.y2 = c * self.y + (1 - c) * (1 - self.y)
        self.x2 = (1 - c) * self.x + c * (1 - self.x)
        self.y3 = (1 - c) * self.y + c * (1 - self.y)
        self.x3 = c * self.x + (1 - c) * (1 - self.x)

    def id(self, z, y, x, c):
        return (z * Y_CHIPS + y, x * CORES + c)

    def z_at(self, k):
        return (self.z - k + self.depth) % self.depth


class Stream:
    def __init__(self, place, buf, width, sems):
        self.p, self.buf, self.width, self.sems = place, buf, width, sems
        self.n = place.depth
        self.sends = []

    def block(self, z, y, x, c):
        rows = pl.multiple_of((x * CORES + c) * self.width, self.width)
        return self.buf.at[z * Y_CHIPS + y, pl.ds(rows, self.width), :]

    def copy(self, kind, index, where, target):
        ref = self.block(*where)
        send, recv = self.sems[kind]
        return pltpu.make_async_remote_copy(
            src_ref=ref,
            dst_ref=ref,
            send_sem=send.at[index],
            recv_sem=recv.at[index],
            device_id=target,
            device_id_type=MESH,
        )

    def send(self, kind, index, where, target):
        copy = self.copy(kind, index, where, target)
        copy.start()
        self.sends.append(copy)

    def arrive(self, kind, index, where):
        p = self.p
        self.copy(kind, index, where, p.id(p.z, p.y, p.x, 1 - p.c)).wait_recv()

    def to_second(self, k, where):
        p = self.p
        self.send("second", k, where, p.id(p.z, p.y2, p.x2, p.c))

    def to_third(self, k, where):
        p = self.p
        self.send("third", k, where, p.id(p.z, p.y3, p.x3, p.c))

    def to_sibling(self, k, where):
        p = self.p
        self.send("sibling", k, where, p.id(p.z, p.y, p.x, 1 - p.c))

    def start(self):
        p = self.p
        own = (p.z, p.y, p.x, p.c)
        for k in range(1, self.n):
            self.send("line", k - 1, own, p.id((p.z + k) % self.n, p.y, p.x, p.c))
        self.to_second(0, own)
        self.to_third(0, own)
        self.to_sibling(0, own)

    def line(self, k):
        p = self.p
        where = (p.z_at(k), p.y, p.x, p.c)
        self.arrive("line", k - 1, where)
        self.to_second(k, where)
        self.to_third(k, where)
        self.to_sibling(k, where)

    def second(self, k):
        p = self.p
        where = (p.z_at(k), p.y2, p.x2, p.c)
        self.arrive("second", k, where)
        self.to_third(self.n + k, where)
        self.to_sibling(self.n + k, where)

    def third(self, k):
        p = self.p
        if k < self.n:
            where = (p.z_at(k), p.y3, p.x3, p.c)
        else:
            where = (p.z_at(k - self.n), 1 - p.y, 1 - p.x, p.c)
        self.arrive("third", k, where)
        self.to_sibling(2 * self.n + k, where)

    def sibling(self):
        p = self.p
        o = 1 - p.c
        y2, x2, y3, x3 = p.y3, p.x3, p.y2, p.x2
        for k in range(self.n):
            self.arrive("sibling", k, (p.z_at(k), p.y, p.x, o))
        for k in range(self.n):
            self.arrive("sibling", self.n + k, (p.z_at(k), y2, x2, o))
        for k in range(self.n):
            self.arrive("sibling", 2 * self.n + k, (p.z_at(k), y3, x3, o))
        for k in range(self.n):
            self.arrive("sibling", 3 * self.n + k, (p.z_at(k), 1 - p.y, 1 - p.x, o))

    def finish(self):
        for copy in self.sends:
            copy.wait_send()


def cov_rows(buf, cov, i):
    slabs, d, _ = buf.shape
    tile = d // TILES
    left = jnp.concatenate([buf[k, i * tile : (i + 1) * tile, :] for k in range(slabs)], axis=1)

    def column(j, carry):
        first = pl.multiple_of(j * tile, tile)
        right = jnp.concatenate([buf[k, pl.ds(first, tile), :] for k in range(slabs)], axis=1)
        cov[i * tile : (i + 1) * tile, pl.ds(first, tile)] = dot_nt(left, right)
        return carry

    lax.fori_loop(0, TILES, column, 0)


def damp(cov, factor, damping):
    d = cov.shape[0]
    step = d // 9
    trace = jnp.zeros((1, 1), F32)
    for i in range(9):
        part = cov[i * step : (i + 1) * step, i * step : (i + 1) * step]
        trace = trace + total(jnp.where(eye(step, step, 0, 0), part, 0.0))
    shift = damping * trace / d

    def rows(i, acc):
        first = pl.multiple_of(i * step, step)
        piece = cov[pl.ds(first, step), :]
        diag = eye(step, d, first, 0)
        piece = (piece + jnp.where(diag, shift, 0.0)).astype(BF16)
        factor[pl.ds(first, step), :] = piece
        wide = piece.astype(F32)
        return acc + jnp.sum(wide * wide, axis=0, keepdims=True)

    squares = lax.fori_loop(0, 9, rows, jnp.zeros((1, d), F32))
    return jnp.sqrt(jnp.sum(squares, axis=1, keepdims=True))


def horner_rows(factor, work, coeffs, first, norm):
    rows, d = work.shape
    tile = d // TILES
    terms = coeffs.shape[0]
    inv = 1.0 / norm
    start = pl.multiple_of(first, rows)
    top = jnp.full((1, 1), coeffs[terms - 1], F32).astype(BF16).astype(F32)
    diag = eye(rows, d, first, 0)
    value = jnp.where(diag, coeffs[terms - 2] + coeffs[terms - 1], 0.0)
    work[...] = value - factor[pl.ds(start, rows), :].astype(F32) * top * inv
    for term in range(terms - 3, -1, -1):
        low = work[...].astype(BF16)
        for j in range(TILES):
            cols = slice(j * tile, (j + 1) * tile)
            product = dot_nn(low, factor[:, cols])
            held = jnp.where(eye(rows, tile, first, j * tile), coeffs[term], 0.0)
            work[:, cols] = held + work[:, cols] - product * inv


def step_kernel(
    shards,
    acts_ref,
    grads_ref,
    weight_ref,
    momentum_ref,
    damping_ref,
    coeffs_ref,
    new_momentum_ref,
    gathered_ref,
    acts_all,
    grads_all,
    cov,
    factor,
    grad_work,
    grad_low,
    act_work,
    projected,
    right,
    weight_all,
    shard_sums,
    tensor_sums,
    *sems,
):
    p = Place(shards)
    n = p.depth
    s, t = p.s, p.t
    tensors = grads_all.shape[1] // grads_ref.shape[1]
    width = grads_ref.shape[1]
    barrier = pltpu.get_barrier_semaphore()
    peers = [((s + k) % shards, t) for k in range(1, shards)]
    peers += [(s, (t + k) % tensors) for k in range(1, tensors)]
    for peer in peers:
        pl.semaphore_signal(barrier, inc=1, device_id=peer, device_id_type=MESH)

    kinds = ("line", "second", "third", "sibling")
    pairs = list(zip(sems[0::2], sems[1::2]))
    grads = Stream(p, grads_all, width, dict(zip(kinds, pairs[0:4])))
    acts = Stream(p, acts_all, width, dict(zip(kinds, pairs[4:8])))
    ones = eye(width, width, 0, 0).astype(F32).astype(BF16)
    own_rows = pl.ds(pl.multiple_of(t * width, width), width)
    grads_all[s, own_rows, :] = dot_nt(ones, grads_ref[...]).astype(BF16)
    acts_all[s, own_rows, :] = dot_nt(ones, acts_ref[...]).astype(BF16)
    pl.semaphore_wait(barrier, len(peers))

    grads.start()
    for k in range(1, n):
        grads.line(k)
        grads.second(k - 1)
    grads.second(n - 1)
    acts.start()
    for k in range(1, n):
        acts.line(k)
        acts.second(k - 1)
        grads.third(2 * k - 2)
        grads.third(2 * k - 1)
    acts.second(n - 1)
    for k in range(2 * n - 2, 2 * n):
        grads.third(k)
    grads.sibling()
    third = 0
    for i in range(TILES):
        cov_rows(grads_all, cov, i)
        acts.third(third)
        third += 1
    grad_norm = damp(cov, factor, damping_ref[1])
    while third < n:
        acts.third(third)
        third += 1
    horner_rows(factor, grad_work, coeffs_ref, t * width, grad_norm)
    grad_low[...] = grad_work[...].astype(BF16)
    acts.third(third)
    third += 1

    def project(k, carry):
        projected[k] = dot_nn(grad_low[...], grads_all[k]).astype(BF16)
        return carry

    lax.fori_loop(0, shards, project, 0)
    while third < 2 * n:
        acts.third(third)
        third += 1
    acts.sibling()
    for i in range(TILES):
        cov_rows(acts_all, cov, i)
    act_norm = damp(cov, factor, damping_ref[0])
    height = weight_ref.shape[0]
    horner_rows(factor, act_work, coeffs_ref, s * height, act_norm)
    tile = cov.shape[0] // TILES
    low = jnp.concatenate([projected[k] for k in range(shards)], axis=1)

    def right_rows(i, carry):
        first = pl.multiple_of(i * tile, tile)
        left = jnp.concatenate(
            [acts_all[k, pl.ds(first, tile), :] for k in range(shards)], axis=1
        )
        right[pl.ds(first, tile), :] = dot_nt(left, low)
        return carry

    lax.fori_loop(0, TILES, right_rows, 0)
    update = dot_nn(act_work[...], right[...], lax.Precision.HIGHEST)

    started = []

    def push(src, dst, pair, index, target):
        copy = pltpu.make_async_remote_copy(
            src_ref=src,
            dst_ref=dst,
            send_sem=pair[0].at[index],
            recv_sem=pair[1].at[index],
            device_id=target,
            device_id_type=MESH,
        )
        copy.start()
        started.append(copy)
        return copy

    shard_sums[s] = jnp.broadcast_to(total(update * update), shard_sums.shape[1:])
    copies = [
        push(shard_sums.at[s], shard_sums.at[s], pairs[8], k - 1, ((s + k) % shards, t))
        for k in range(1, shards)
    ]
    for copy in copies:
        copy.wait_recv()
    tensor_sums[t] = jnp.sum(shard_sums[...], axis=0)
    copies = [
        push(tensor_sums.at[t], tensor_sums.at[t], pairs[9], k - 1, (s, (t + k) % tensors))
        for k in range(1, tensors)
    ]
    for copy in copies:
        copy.wait_recv()
    square_sum = jnp.sum(tensor_sums[...], axis=0)[0:1, 0:1]
    d = cov.shape[0]
    mean_square = square_sum / (d * d)
    momentum = 0.9 * momentum_ref[...] + update / jnp.sqrt(mean_square + 1e-06)
    new_momentum_ref[...] = momentum
    new_weight = weight_ref[...].astype(F32) - 0.1 * momentum

    def rows_of(z, y):
        return weight_all.at[pl.ds(pl.multiple_of((z * Y_CHIPS + y) * height, height), height), :]

    weight_all[pl.ds(pl.multiple_of(s * height, height), height), :] = new_weight.astype(BF16)
    own = rows_of(p.z, p.y)
    across = (p.z * Y_CHIPS + 1 - p.y, t)
    lines = [
        push(own, own, pairs[10], k - 1, (((p.z + k) % n) * Y_CHIPS + p.y, t))
        for k in range(1, n)
    ]
    crossed = [push(own, own, pairs[11], 0, across)]
    for k in range(1, n):
        lines[k - 1].wait_recv()
        piece = rows_of(p.z_at(k), p.y)
        crossed.append(push(piece, piece, pairs[11], k, across))
    for copy in crossed:
        copy.wait_recv()
    gathered_ref[...] = weight_all[...]
    for copy in started:
        copy.wait_send()
    grads.finish()
    acts.finish()


def on_device_whole(shards, tensors, acts, outgrads, weight, momentum, damping, coeffs):
    tokens, width = acts.shape
    height = weight.shape[0]
    d = width * tensors
    n = shards // Y_CHIPS
    vmem = pl.BlockSpec(memory_space=pltpu.VMEM)
    smem = pl.BlockSpec(memory_space=pltpu.SMEM)
    counts = [n - 1, n, 2 * n, 4 * n] * 2 + [shards - 1, tensors - 1, n - 1, n]
    sems = []
    for count in counts:
        sems += [pltpu.SemaphoreType.DMA((count,))] * 2
    return pl.pallas_call(
        functools.partial(step_kernel, shards),
        out_shape=(
            jax.ShapeDtypeStruct((height, width), F32),
            jax.ShapeDtypeStruct((d, width), BF16),
        ),
        in_specs=[vmem, vmem, vmem, vmem, smem, smem],
        out_specs=(vmem, vmem),
        scratch_shapes=[
            pltpu.VMEM((shards, d, tokens), BF16),
            pltpu.VMEM((shards, d, tokens), BF16),
            pltpu.VMEM((d, d), F32),
            pltpu.VMEM((d, d), BF16),
            pltpu.VMEM((width, d), F32),
            pltpu.VMEM((width, d), BF16),
            pltpu.VMEM((height, d), F32),
            pltpu.VMEM((shards, width, tokens), BF16),
            pltpu.VMEM((d, width), F32),
            pltpu.VMEM((d, width), BF16),
            pltpu.VMEM((shards, 8, 128), F32),
            pltpu.VMEM((tensors, 8, 128), F32),
        ]
        + sems,
        compiler_params=pltpu.CompilerParams(
            collective_id=0, has_side_effects=True, vmem_limit_bytes=56 * 2**20
        ),
    )(acts, outgrads, weight, momentum, damping, coeffs)


def solution(mesh):
    in_specs = (
        P("shard", "tensor"),
        P("shard", "tensor"),
        P("shard", "tensor"),
        P("shard", "tensor"),
        P(),
        P(),
    )
    out_specs = (P("shard", "tensor"), P(None, "tensor"))
    shards, tensors = mesh.shape["shard"], mesh.shape["tensor"]

    def local(acts, *rest):
        held = 2 * acts.dtype.itemsize * acts.size * shards * tensors
        if held <= 24 * 2**20:
            return on_device_whole(shards, tensors, acts, *rest)
        return on_device(acts, *rest)

    return jax.shard_map(
        local, mesh=mesh, in_specs=in_specs, out_specs=out_specs, check_vma=False
    )
```

```python
import functools

import jax
import jax.numpy as jnp
from jax import lax
from jax.experimental import pallas as pl
from jax.experimental.pallas import tpu as pltpu
from jax.sharding import PartitionSpec as P

D = 1152


def horner_columns(factor, coeffs, first_col, col_count, bound_norm):
    extent = factor.shape[0]
    row_ids = lax.broadcasted_iota(jnp.int32, (extent, col_count), 0)
    col_ids = lax.broadcasted_iota(jnp.int32, (extent, col_count), 1) + first_col
    identity_cols = (row_ids == col_ids).astype(jnp.float32)
    term_count = coeffs.shape[0]
    iterate = coeffs[term_count - 1] * identity_cols
    for term_index in range(term_count - 2, -1, -1):
        product = jnp.dot(factor, iterate.astype(jnp.bfloat16), preferred_element_type=jnp.float32)
        iterate = coeffs[term_index] * identity_cols + iterate - product / bound_norm
    return iterate


def tokens_product(left, right):
    return lax.dot_general(
        left, right, (((0,), (0,)), ((), ())), preferred_element_type=jnp.float32
    )


def on_device(acts, outgrads, weight, momentum, damping, coeffs):
    row_count = weight.shape[0]
    col_count = weight.shape[1]
    row_first = lax.axis_index("shard") * row_count
    col_first = lax.axis_index("tensor") * col_count
    full_acts, full_grads = (
        lax.all_gather(acts, "tensor", axis=1, tiled=True),
        lax.all_gather(outgrads, "tensor", axis=1, tiled=True),
    )
    local_squares = jnp.stack(
        [
            jnp.sum(jnp.square(acts.astype(jnp.float32))),
            jnp.sum(jnp.square(outgrads.astype(jnp.float32))),
        ]
    )
    traces = lax.psum(local_squares, ("shard", "tensor"))
    act_part = tokens_product(full_acts, acts)
    grad_part = tokens_product(full_grads, outgrads)
    stats = lax.psum_scatter(
        jnp.concatenate([act_part, grad_part], axis=1), "shard", scatter_dimension=0, tiled=True
    )
    row_ids = lax.broadcasted_iota(jnp.int32, (row_count, col_count), 0) + row_first
    col_ids = lax.broadcasted_iota(jnp.int32, (row_count, col_count), 1) + col_first
    diag_mask = (row_ids == col_ids).astype(jnp.float32)
    act_piece = (stats[:, :col_count] + damping[0] * traces[0] / D * diag_mask).astype(jnp.bfloat16)
    grad_piece = (stats[:, col_count:] + damping[1] * traces[1] / D * diag_mask).astype(
        jnp.bfloat16
    )
    act_wide, grad_wide = (
        lax.all_gather(act_piece, "tensor", axis=1, tiled=True),
        lax.all_gather(grad_piece, "tensor", axis=1, tiled=True),
    )
    act_full, grad_full = (
        lax.all_gather(act_wide, "shard", axis=0, tiled=True),
        lax.all_gather(grad_wide, "shard", axis=0, tiled=True),
    )
    act_scale = jnp.sqrt(jnp.sum(jnp.square(act_full.astype(jnp.float32))))
    grad_scale = jnp.sqrt(jnp.sum(jnp.square(grad_full.astype(jnp.float32))))
    act_inverse = horner_columns(act_full, coeffs, row_first, row_count, act_scale)
    grad_inverse = horner_columns(grad_full, coeffs, col_first, col_count, grad_scale).astype(
        jnp.bfloat16
    )
    projected = jnp.dot(full_grads, grad_inverse, preferred_element_type=jnp.float32).astype(
        jnp.bfloat16
    )
    right_term = tokens_product(full_acts, projected)
    right_product = lax.psum(right_term, "shard")
    update = lax.dot_general(
        act_inverse,
        right_product,
        (((0,), (0,)), ((), ())),
        precision=lax.Precision.HIGHEST,
        preferred_element_type=jnp.float32,
    )
    square_sum = lax.psum(jnp.sum(update * update), ("shard", "tensor"))
    mean_square = square_sum / (D * D)
    new_momentum = 0.9 * momentum + update / jnp.sqrt(mean_square + 1e-06)
    new_weight = (weight.astype(jnp.float32) - 0.1 * new_momentum).astype(jnp.bfloat16)
    gathered_weight = lax.all_gather(new_weight, "shard", axis=0, tiled=True)
    return (new_momentum, gathered_weight)


MESH = pl.DeviceIdType.MESH
BF16 = jnp.bfloat16
F32 = jnp.float32
Y_CHIPS = 2
CORES = 2
TILES = 3


def dot_nt(left, right):
    return lax.dot_general(
        left, right, (((1,), (1,)), ((), ())), preferred_element_type=jnp.float32
    )


def dot_nn(left, right, precision=None):
    return lax.dot_general(
        left,
        right,
        (((1,), (0,)), ((), ())),
        precision=precision,
        preferred_element_type=jnp.float32,
    )


def eye(rows, cols, row_first, col_first):
    row_ids = lax.broadcasted_iota(jnp.int32, (rows, cols), 0) + row_first
    col_ids = lax.broadcasted_iota(jnp.int32, (rows, cols), 1) + col_first
    return row_ids == col_ids


def total(value):
    return jnp.sum(jnp.sum(value, axis=0, keepdims=True), axis=1, keepdims=True)


class Place:
    def __init__(self, shards):
        self.depth = shards // Y_CHIPS
        self.s = lax.axis_index("shard")
        self.t = lax.axis_index("tensor")
        self.z, self.y = self.s // Y_CHIPS, self.s % Y_CHIPS
        self.x, self.c = self.t // CORES, self.t % CORES
        c = self.c
        self.y2 = c * self.y + (1 - c) * (1 - self.y)
        self.x2 = (1 - c) * self.x + c * (1 - self.x)
        self.y3 = (1 - c) * self.y + c * (1 - self.y)
        self.x3 = c * self.x + (1 - c) * (1 - self.x)

    def id(self, z, y, x, c):
        return (z * Y_CHIPS + y, x * CORES + c)

    def z_at(self, k):
        return (self.z - k + self.depth) % self.depth


class Stream:
    def __init__(self, place, buf, width, sems):
        self.p, self.buf, self.width, self.sems = place, buf, width, sems
        self.n = place.depth
        self.sends = []

    def block(self, z, y, x, c):
        rows = pl.multiple_of((x * CORES + c) * self.width, self.width)
        return self.buf.at[z * Y_CHIPS + y, pl.ds(rows, self.width), :]

    def copy(self, kind, index, where, target):
        ref = self.block(*where)
        send, recv = self.sems[kind]
        return pltpu.make_async_remote_copy(
            src_ref=ref,
            dst_ref=ref,
            send_sem=send.at[index],
            recv_sem=recv.at[index],
            device_id=target,
            device_id_type=MESH,
        )

    def send(self, kind, index, where, target):
        copy = self.copy(kind, index, where, target)
        copy.start()
        self.sends.append(copy)

    def arrive(self, kind, index, where):
        p = self.p
        self.copy(kind, index, where, p.id(p.z, p.y, p.x, 1 - p.c)).wait_recv()

    def to_second(self, k, where):
        p = self.p
        self.send("second", k, where, p.id(p.z, p.y2, p.x2, p.c))

    def to_third(self, k, where):
        p = self.p
        self.send("third", k, where, p.id(p.z, p.y3, p.x3, p.c))

    def to_sibling(self, k, where):
        p = self.p
        self.send("sibling", k, where, p.id(p.z, p.y, p.x, 1 - p.c))

    def start(self):
        p = self.p
        own = (p.z, p.y, p.x, p.c)
        for k in range(1, self.n):
            self.send("line", k - 1, own, p.id((p.z + k) % self.n, p.y, p.x, p.c))
        self.to_second(0, own)
        self.to_third(0, own)
        self.to_sibling(0, own)

    def line(self, k):
        p = self.p
        where = (p.z_at(k), p.y, p.x, p.c)
        self.arrive("line", k - 1, where)
        self.to_second(k, where)
        self.to_third(k, where)
        self.to_sibling(k, where)

    def second(self, k):
        p = self.p
        where = (p.z_at(k), p.y2, p.x2, p.c)
        self.arrive("second", k, where)
        self.to_third(self.n + k, where)
        self.to_sibling(self.n + k, where)

    def third(self, k):
        p = self.p
        if k < self.n:
            where = (p.z_at(k), p.y3, p.x3, p.c)
        else:
            where = (p.z_at(k - self.n), 1 - p.y, 1 - p.x, p.c)
        self.arrive("third", k, where)
        self.to_sibling(2 * self.n + k, where)

    def sibling(self, first, last):
        p = self.p
        where = [(p.y, p.x), (p.y3, p.x3), (p.y2, p.x2), (1 - p.y, 1 - p.x)]
        for k in range(first, last):
            y, x = where[k // self.n]
            self.arrive("sibling", k, (p.z_at(k % self.n), y, x, 1 - p.c))

    def finish(self):
        for copy in self.sends:
            copy.wait_send()


def lanes(buf, slabs, rows):
    return jnp.concatenate([buf[k, rows, :] for k in slabs], axis=1)


def cov_tile(buf, cov, slabs, i, j, add):
    tile = cov.shape[0] // TILES
    rows, cols = pl.ds(i * tile, tile), pl.ds(j * tile, tile)
    product = dot_nt(lanes(buf, slabs, rows), lanes(buf, slabs, cols))
    cov[rows, cols] = cov[rows, cols] + product if add else product


def damp(cov, factor, damping):
    d = cov.shape[0]
    step = d // 9
    trace = jnp.zeros((1, 1), F32)
    for i in range(9):
        part = cov[i * step : (i + 1) * step, i * step : (i + 1) * step]
        trace = trace + total(jnp.where(eye(step, step, 0, 0), part, 0.0))
    shift = damping * trace / d

    def rows(i, acc):
        first = pl.multiple_of(i * step, step)
        piece = cov[pl.ds(first, step), :]
        diag = eye(step, d, first, 0)
        piece = (piece + jnp.where(diag, shift, 0.0)).astype(BF16)
        factor[pl.ds(first, step), :] = piece
        wide = piece.astype(F32)
        return acc + jnp.sum(wide * wide, axis=0, keepdims=True)

    squares = lax.fori_loop(0, 9, rows, jnp.zeros((1, d), F32))
    return jnp.sqrt(jnp.sum(squares, axis=1, keepdims=True))


def horner_steps(factor, work, coeffs, first, norm):
    rows, d = work.shape
    tile = d // TILES
    terms = coeffs.shape[0]

    def begin():
        start = pl.multiple_of(first, rows)
        top = jnp.full((1, 1), coeffs[terms - 1], F32).astype(BF16).astype(F32)
        diag = eye(rows, d, first, 0)
        value = jnp.where(diag, coeffs[terms - 2] + coeffs[terms - 1], 0.0)
        work[...] = value - factor[pl.ds(start, rows), :].astype(F32) * (top / norm())

    def term(index):
        low = work[...].astype(BF16)
        inv = 1.0 / norm()
        for j in range(TILES):
            cols = slice(j * tile, (j + 1) * tile)
            product = dot_nn(low, factor[:, cols])
            held = jnp.where(eye(rows, tile, first, j * tile), coeffs[index], 0.0)
            work[:, cols] = held + work[:, cols] - product * inv

    return [begin] + [functools.partial(term, k) for k in range(terms - 3, -1, -1)]


def step_kernel(
    shards,
    acts_ref,
    grads_ref,
    weight_ref,
    momentum_ref,
    damping_ref,
    coeffs_ref,
    new_momentum_ref,
    gathered_ref,
    acts_all,
    grads_all,
    cov,
    factor,
    grad_work,
    grad_low,
    act_work,
    projected,
    right,
    weight_all,
    shard_sums,
    tensor_sums,
    *sems,
):
    p = Place(shards)
    n = p.depth
    s, t = p.s, p.t
    tensors = grads_all.shape[1] // grads_ref.shape[0]
    width = grads_ref.shape[0]
    barrier = pltpu.get_barrier_semaphore()
    peers = [((s + k) % shards, t) for k in range(1, shards)]
    peers += [(s, (t + k) % tensors) for k in range(1, tensors)]
    for peer in peers:
        pl.semaphore_signal(barrier, inc=1, device_id=peer, device_id_type=MESH)

    kinds = ("line", "second", "third", "sibling")
    pairs = list(zip(sems[0::2], sems[1::2]))
    grads = Stream(p, grads_all, width, dict(zip(kinds, pairs[0:4])))
    acts = Stream(p, acts_all, width, dict(zip(kinds, pairs[4:8])))
    own_rows = pl.ds(pl.multiple_of(t * width, width), width)
    grads_all[s, own_rows, :] = grads_ref[...]
    acts_all[s, own_rows, :] = acts_ref[...]
    pl.semaphore_wait(barrier, len(peers))

    grads.start()
    for k in range(1, n):
        grads.line(k)
        grads.second(k - 1)
    grads.second(n - 1)
    for k in range(n):
        grads.third(k)
    acts.start()
    for k in range(n, 2 * n):
        grads.third(k)
    grads.sibling(0, 4 * n)

    every = range(shards)
    norms = {}

    def damp_grads():
        norms["grads"] = damp(cov, factor, damping_ref[1])

    def project(k):
        projected[k] = dot_nn(grad_low[...], grads_all[k]).astype(BF16)

    def lower():
        grad_low[...] = grad_work[...].astype(BF16)

    work = [
        functools.partial(cov_tile, grads_all, cov, every, i, j, False)
        for i in range(TILES)
        for j in range(TILES)
    ]
    work += [damp_grads]
    work += horner_steps(factor, grad_work, coeffs_ref, t * width, lambda: norms["grads"])
    work += [lower]
    work += [functools.partial(project, k) for k in every]
    relays = []
    for k in range(1, n):
        relays += [functools.partial(acts.line, k), functools.partial(acts.second, k - 1)]
    relays += [functools.partial(acts.second, n - 1)]
    relays += [functools.partial(acts.third, k) for k in range(n)]
    done = 0
    for index, chunk in enumerate(work):
        chunk()
        upto = (index + 1) * len(relays) // len(work)
        for relay in relays[done:upto]:
            relay()
        done = upto
    near = [2 * k + p.y for k in range(n)]
    far = [2 * k + 1 - p.y for k in range(n)]
    acts.sibling(0, 3 * n)
    tile = cov.shape[0] // TILES

    def right_rows(slabs, i, add):
        rows = pl.ds(i * tile, tile)
        low = jnp.concatenate([projected[k] for k in slabs], axis=1)
        product = dot_nt(lanes(acts_all, slabs, rows), low)
        right[rows, :] = right[rows, :] + product if add else product

    third = n
    for i in range(TILES):
        for j in range(TILES):
            cov_tile(acts_all, cov, near, i, j, False)
            if j % 2 == 1 and third < 2 * n:
                acts.third(third)
                third += 1
        right_rows(near, i, False)
    while third < 2 * n:
        acts.third(third)
        third += 1
    acts.sibling(3 * n, 4 * n)
    for i in range(TILES):
        for j in range(TILES):
            cov_tile(acts_all, cov, far, i, j, True)
    act_norm = damp(cov, factor, damping_ref[0])
    height = weight_ref.shape[0]
    for run in horner_steps(factor, act_work, coeffs_ref, s * height, lambda: act_norm):
        run()
    for i in range(TILES):
        right_rows(far, i, True)
    update = dot_nn(act_work[...], right[...], lax.Precision.HIGHEST)

    started = []

    def push(src, dst, pair, index, target):
        copy = pltpu.make_async_remote_copy(
            src_ref=src,
            dst_ref=dst,
            send_sem=pair[0].at[index],
            recv_sem=pair[1].at[index],
            device_id=target,
            device_id_type=MESH,
        )
        copy.start()
        started.append(copy)
        return copy

    shard_sums[s] = jnp.broadcast_to(total(update * update), shard_sums.shape[1:])
    copies = [
        push(shard_sums.at[s], shard_sums.at[s], pairs[8], k - 1, ((s + k) % shards, t))
        for k in range(1, shards)
    ]
    for copy in copies:
        copy.wait_recv()
    tensor_sums[t] = jnp.sum(shard_sums[...], axis=0)
    copies = [
        push(tensor_sums.at[t], tensor_sums.at[t], pairs[9], k - 1, (s, (t + k) % tensors))
        for k in range(1, tensors)
    ]
    for copy in copies:
        copy.wait_recv()
    square_sum = jnp.sum(tensor_sums[...], axis=0)[0:1, 0:1]
    d = cov.shape[0]
    mean_square = square_sum / (d * d)
    momentum = 0.9 * momentum_ref[...] + update / jnp.sqrt(mean_square + 1e-06)
    new_momentum_ref[...] = momentum
    new_weight = weight_ref[...].astype(F32) - 0.1 * momentum

    low = new_weight.astype(BF16)
    main = weight_all.shape[2]
    rest = width - main
    weight_all[s, :height, :] = low[:, :main]
    ones = eye(rest, rest, 0, 0).astype(F32).astype(BF16)
    weight_all[s, height:, :height] = dot_nt(ones, low[:, main:]).astype(BF16)

    def rows_of(z, y):
        return weight_all.at[z * Y_CHIPS + y]

    own = rows_of(p.z, p.y)
    across = (p.z * Y_CHIPS + 1 - p.y, t)
    lines = [
        push(own, own, pairs[10], k - 1, (((p.z + k) % n) * Y_CHIPS + p.y, t))
        for k in range(1, n)
    ]
    crossed = [push(own, own, pairs[11], 0, across)]
    for k in range(1, n):
        lines[k - 1].wait_recv()
        piece = rows_of(p.z_at(k), p.y)
        crossed.append(push(piece, piece, pairs[11], k, across))
    for copy in crossed:
        copy.wait_recv()
    rows = jnp.concatenate([weight_all[k, :height, :] for k in range(shards)], axis=0)
    ones = eye(main, main, 0, 0).astype(F32).astype(BF16)
    gathered_ref[:main, :] = dot_nt(ones, rows).astype(BF16)
    for k in range(shards):
        gathered_ref[main:, k * height : (k + 1) * height] = weight_all[k, height:, :height]
    for copy in started:
        copy.wait_send()
    grads.finish()
    acts.finish()


def on_device_whole(shards, tensors, acts, outgrads, weight, momentum, damping, coeffs):
    tokens, width = acts.shape
    height = weight.shape[0]
    d = width * tensors
    n = shards // Y_CHIPS
    vmem = pl.BlockSpec(memory_space=pltpu.VMEM)
    smem = pl.BlockSpec(memory_space=pltpu.SMEM)
    counts = [n - 1, n, 2 * n, 4 * n] * 2 + [shards - 1, tensors - 1, n - 1, n]
    sems = []
    for count in counts:
        sems += [pltpu.SemaphoreType.DMA((count,))] * 2
    new_momentum, gathered = pl.pallas_call(
        functools.partial(step_kernel, shards),
        out_shape=(
            jax.ShapeDtypeStruct((height, width), F32),
            jax.ShapeDtypeStruct((width, d), BF16),
        ),
        in_specs=[vmem, vmem, vmem, vmem, smem, smem],
        out_specs=(vmem, vmem),
        scratch_shapes=[
            pltpu.VMEM((shards, d, tokens), BF16),
            pltpu.VMEM((shards, d, tokens), BF16),
            pltpu.VMEM((d, d), F32),
            pltpu.VMEM((d, d), BF16),
            pltpu.VMEM((width, d), F32),
            pltpu.VMEM((width, d), BF16),
            pltpu.VMEM((height, d), F32),
            pltpu.VMEM((shards, width, tokens), BF16),
            pltpu.VMEM((d, width), F32),
            pltpu.VMEM((shards, height + width % 128, width // 128 * 128), BF16),
            pltpu.VMEM((shards, 8, 128), F32),
            pltpu.VMEM((tensors, 8, 128), F32),
        ]
        + sems,
        compiler_params=pltpu.CompilerParams(
            collective_id=0, has_side_effects=True, vmem_limit_bytes=56 * 2**20
        ),
    )(acts.T, outgrads.T, weight, momentum, damping, coeffs)
    return new_momentum, gathered.T


def solution(mesh):
    in_specs = (
        P("shard", "tensor"),
        P("shard", "tensor"),
        P("shard", "tensor"),
        P("shard", "tensor"),
        P(),
        P(),
    )
    out_specs = (P("shard", "tensor"), P(None, "tensor"))
    shards, tensors = mesh.shape["shard"], mesh.shape["tensor"]

    def local(acts, *rest):
        held = 2 * acts.dtype.itemsize * acts.size * shards * tensors
        if held <= 24 * 2**20:
            return on_device_whole(shards, tensors, acts, *rest)
        return on_device(acts, *rest)

    return jax.shard_map(
        local, mesh=mesh, in_specs=in_specs, out_specs=out_specs, check_vma=False
    )
```

```python
import functools

import jax
import jax.numpy as jnp
from jax import lax
from jax.experimental import pallas as pl
from jax.experimental.pallas import tpu as pltpu
from jax.sharding import PartitionSpec as P

D = 1152


def horner_columns(factor, coeffs, first_col, col_count, bound_norm):
    extent = factor.shape[0]
    row_ids = lax.broadcasted_iota(jnp.int32, (extent, col_count), 0)
    col_ids = lax.broadcasted_iota(jnp.int32, (extent, col_count), 1) + first_col
    identity_cols = (row_ids == col_ids).astype(jnp.float32)
    term_count = coeffs.shape[0]
    iterate = coeffs[term_count - 1] * identity_cols
    for term_index in range(term_count - 2, -1, -1):
        product = jnp.dot(factor, iterate.astype(jnp.bfloat16), preferred_element_type=jnp.float32)
        iterate = coeffs[term_index] * identity_cols + iterate - product / bound_norm
    return iterate


def tokens_product(left, right):
    return lax.dot_general(
        left, right, (((0,), (0,)), ((), ())), preferred_element_type=jnp.float32
    )


def on_device(acts, outgrads, weight, momentum, damping, coeffs):
    row_count = weight.shape[0]
    col_count = weight.shape[1]
    row_first = lax.axis_index("shard") * row_count
    col_first = lax.axis_index("tensor") * col_count
    full_acts, full_grads = (
        lax.all_gather(acts, "tensor", axis=1, tiled=True),
        lax.all_gather(outgrads, "tensor", axis=1, tiled=True),
    )
    local_squares = jnp.stack(
        [
            jnp.sum(jnp.square(acts.astype(jnp.float32))),
            jnp.sum(jnp.square(outgrads.astype(jnp.float32))),
        ]
    )
    traces = lax.psum(local_squares, ("shard", "tensor"))
    act_part = tokens_product(full_acts, acts)
    grad_part = tokens_product(full_grads, outgrads)
    stats = lax.psum_scatter(
        jnp.concatenate([act_part, grad_part], axis=1), "shard", scatter_dimension=0, tiled=True
    )
    row_ids = lax.broadcasted_iota(jnp.int32, (row_count, col_count), 0) + row_first
    col_ids = lax.broadcasted_iota(jnp.int32, (row_count, col_count), 1) + col_first
    diag_mask = (row_ids == col_ids).astype(jnp.float32)
    act_piece = (stats[:, :col_count] + damping[0] * traces[0] / D * diag_mask).astype(jnp.bfloat16)
    grad_piece = (stats[:, col_count:] + damping[1] * traces[1] / D * diag_mask).astype(
        jnp.bfloat16
    )
    act_wide, grad_wide = (
        lax.all_gather(act_piece, "tensor", axis=1, tiled=True),
        lax.all_gather(grad_piece, "tensor", axis=1, tiled=True),
    )
    act_full, grad_full = (
        lax.all_gather(act_wide, "shard", axis=0, tiled=True),
        lax.all_gather(grad_wide, "shard", axis=0, tiled=True),
    )
    act_scale = jnp.sqrt(jnp.sum(jnp.square(act_full.astype(jnp.float32))))
    grad_scale = jnp.sqrt(jnp.sum(jnp.square(grad_full.astype(jnp.float32))))
    act_inverse = horner_columns(act_full, coeffs, row_first, row_count, act_scale)
    grad_inverse = horner_columns(grad_full, coeffs, col_first, col_count, grad_scale).astype(
        jnp.bfloat16
    )
    projected = jnp.dot(full_grads, grad_inverse, preferred_element_type=jnp.float32).astype(
        jnp.bfloat16
    )
    right_term = tokens_product(full_acts, projected)
    right_product = lax.psum(right_term, "shard")
    update = lax.dot_general(
        act_inverse,
        right_product,
        (((0,), (0,)), ((), ())),
        precision=lax.Precision.HIGHEST,
        preferred_element_type=jnp.float32,
    )
    square_sum = lax.psum(jnp.sum(update * update), ("shard", "tensor"))
    mean_square = square_sum / (D * D)
    new_momentum = 0.9 * momentum + update / jnp.sqrt(mean_square + 1e-06)
    new_weight = (weight.astype(jnp.float32) - 0.1 * new_momentum).astype(jnp.bfloat16)
    gathered_weight = lax.all_gather(new_weight, "shard", axis=0, tiled=True)
    return (new_momentum, gathered_weight)


MESH = pl.DeviceIdType.MESH
BF16 = jnp.bfloat16
F32 = jnp.float32
Y_CHIPS = 2
CORES = 2
TILES = 3


def dot_nt(left, right):
    return lax.dot_general(
        left, right, (((1,), (1,)), ((), ())), preferred_element_type=jnp.float32
    )


def dot_nn(left, right, precision=None):
    return lax.dot_general(
        left,
        right,
        (((1,), (0,)), ((), ())),
        precision=precision,
        preferred_element_type=jnp.float32,
    )


def eye(rows, cols, row_first, col_first):
    row_ids = lax.broadcasted_iota(jnp.int32, (rows, cols), 0) + row_first
    col_ids = lax.broadcasted_iota(jnp.int32, (rows, cols), 1) + col_first
    return row_ids == col_ids


def total(value):
    return jnp.sum(jnp.sum(value, axis=0, keepdims=True), axis=1, keepdims=True)


class Place:
    def __init__(self, shards):
        self.depth = shards // Y_CHIPS
        self.s = lax.axis_index("shard")
        self.t = lax.axis_index("tensor")
        self.z, self.y = self.s // Y_CHIPS, self.s % Y_CHIPS
        self.x, self.c = self.t // CORES, self.t % CORES
        c = self.c
        self.y2 = c * self.y + (1 - c) * (1 - self.y)
        self.x2 = (1 - c) * self.x + c * (1 - self.x)
        self.y3 = (1 - c) * self.y + c * (1 - self.y)
        self.x3 = c * self.x + (1 - c) * (1 - self.x)

    def id(self, z, y, x, c):
        return (z * Y_CHIPS + y, x * CORES + c)

    def z_at(self, k):
        return (self.z - k + self.depth) % self.depth


class Stream:
    def __init__(self, place, buf, width, sems):
        self.p, self.buf, self.width, self.sems = place, buf, width, sems
        self.n = place.depth
        self.sends = []

    def block(self, z, y, x, c):
        rows = pl.multiple_of((x * CORES + c) * self.width, self.width)
        return self.buf.at[z * Y_CHIPS + y, pl.ds(rows, self.width), :]

    def copy(self, kind, index, where, target):
        ref = self.block(*where)
        send, recv = self.sems[kind]
        return pltpu.make_async_remote_copy(
            src_ref=ref,
            dst_ref=ref,
            send_sem=send.at[index],
            recv_sem=recv.at[index],
            device_id=target,
            device_id_type=MESH,
        )

    def send(self, kind, index, where, target):
        copy = self.copy(kind, index, where, target)
        copy.start()
        self.sends.append(copy)

    def arrive(self, kind, index, where):
        p = self.p
        self.copy(kind, index, where, p.id(p.z, p.y, p.x, 1 - p.c)).wait_recv()

    def to_second(self, k, where):
        p = self.p
        self.send("second", k, where, p.id(p.z, p.y2, p.x2, p.c))

    def to_third(self, k, where):
        p = self.p
        self.send("third", k, where, p.id(p.z, p.y3, p.x3, p.c))

    def to_sibling(self, k, where):
        p = self.p
        self.send("sibling", k, where, p.id(p.z, p.y, p.x, 1 - p.c))

    def start(self):
        p = self.p
        own = (p.z, p.y, p.x, p.c)
        for k in range(1, self.n):
            self.send("line", k - 1, own, p.id((p.z + k) % self.n, p.y, p.x, p.c))
        self.to_second(0, own)
        self.to_third(0, own)
        self.to_sibling(0, own)

    def line(self, k):
        p = self.p
        where = (p.z_at(k), p.y, p.x, p.c)
        self.arrive("line", k - 1, where)
        self.to_second(k, where)
        self.to_third(k, where)
        self.to_sibling(k, where)

    def second(self, k):
        p = self.p
        where = (p.z_at(k), p.y2, p.x2, p.c)
        self.arrive("second", k, where)
        self.to_third(self.n + k, where)
        self.to_sibling(self.n + k, where)

    def third(self, k):
        p = self.p
        if k < self.n:
            where = (p.z_at(k), p.y3, p.x3, p.c)
        else:
            where = (p.z_at(k - self.n), 1 - p.y, 1 - p.x, p.c)
        self.arrive("third", k, where)
        self.to_sibling(2 * self.n + k, where)

    def sibling(self, first, last):
        p = self.p
        where = [(p.y, p.x), (p.y3, p.x3), (p.y2, p.x2), (1 - p.y, 1 - p.x)]
        for k in range(first, last):
            y, x = where[k // self.n]
            self.arrive("sibling", k, (p.z_at(k % self.n), y, x, 1 - p.c))

    def finish(self):
        for copy in self.sends:
            copy.wait_send()


def lanes(buf, slabs, rows):
    return jnp.concatenate([buf[k, rows, :] for k in slabs], axis=1)


def cov_tile(buf, cov, slabs, i, j, add):
    tile = cov.shape[0] // TILES
    rows, cols = pl.ds(i * tile, tile), pl.ds(j * tile, tile)
    product = dot_nt(lanes(buf, slabs, rows), lanes(buf, slabs, cols))
    cov[rows, cols] = cov[rows, cols] + product if add else product


def damp(cov, factor, damping):
    d = cov.shape[0]
    step = d // 9
    trace = jnp.zeros((1, 1), F32)
    for i in range(9):
        part = cov[i * step : (i + 1) * step, i * step : (i + 1) * step]
        trace = trace + total(jnp.where(eye(step, step, 0, 0), part, 0.0))
    shift = damping * trace / d

    tile = d // TILES
    unit = eye(tile, tile, 0, 0)
    ones = unit.astype(F32).astype(BF16)
    squares = jnp.zeros((1, tile), F32)
    for i in range(TILES):
        for j in range(i, TILES):
            rows, cols = slice(i * tile, (i + 1) * tile), slice(j * tile, (j + 1) * tile)
            piece = cov[rows, cols]
            if i == j:
                piece = piece + jnp.where(unit, shift, 0.0)
            low = piece.astype(BF16)
            factor[rows, cols] = low
            wide = low.astype(F32)
            square = jnp.sum(wide * wide, axis=0, keepdims=True)
            squares = squares + (square if i == j else 2.0 * square)
            if i != j:
                factor[cols, rows] = dot_nt(ones, low).astype(BF16)
    return jnp.sqrt(jnp.sum(squares, axis=1, keepdims=True))


def horner_steps(factor, work, coeffs, first, norm):
    rows, d = work.shape
    tile = d // TILES
    terms = coeffs.shape[0]

    def begin():
        start = pl.multiple_of(first, rows)
        top = jnp.full((1, 1), coeffs[terms - 1], F32).astype(BF16).astype(F32)
        diag = eye(rows, d, first, 0)
        value = jnp.where(diag, coeffs[terms - 2] + coeffs[terms - 1], 0.0)
        work[...] = value - factor[pl.ds(start, rows), :].astype(F32) * (top / norm())

    def term(index):
        low = work[...].astype(BF16)
        inv = 1.0 / norm()
        for j in range(TILES):
            cols = slice(j * tile, (j + 1) * tile)
            product = dot_nn(low, factor[:, cols])
            held = jnp.where(eye(rows, tile, first, j * tile), coeffs[index], 0.0)
            work[:, cols] = held + work[:, cols] - product * inv

    return [begin] + [functools.partial(term, k) for k in range(terms - 3, -1, -1)]


def step_kernel(
    shards,
    acts_ref,
    grads_ref,
    weight_ref,
    momentum_ref,
    damping_ref,
    coeffs_ref,
    new_momentum_ref,
    gathered_ref,
    acts_all,
    grads_all,
    cov,
    factor,
    grad_work,
    grad_low,
    act_work,
    projected,
    right,
    weight_all,
    shard_sums,
    tensor_sums,
    *sems,
):
    p = Place(shards)
    n = p.depth
    s, t = p.s, p.t
    tensors = grads_all.shape[1] // grads_ref.shape[0]
    width = grads_ref.shape[0]
    barrier = pltpu.get_barrier_semaphore()
    peers = [((s + k) % shards, t) for k in range(1, shards)]
    peers += [(s, (t + k) % tensors) for k in range(1, tensors)]
    for peer in peers:
        pl.semaphore_signal(barrier, inc=1, device_id=peer, device_id_type=MESH)

    kinds = ("line", "second", "third", "sibling")
    pairs = list(zip(sems[0::2], sems[1::2]))
    grads = Stream(p, grads_all, width, dict(zip(kinds, pairs[0:4])))
    acts = Stream(p, acts_all, width, dict(zip(kinds, pairs[4:8])))
    own_rows = pl.ds(pl.multiple_of(t * width, width), width)
    grads_all[s, own_rows, :] = grads_ref[...]
    acts_all[s, own_rows, :] = acts_ref[...]
    pl.semaphore_wait(barrier, len(peers))

    grads.start()
    for k in range(1, n):
        grads.line(k)
        grads.second(k - 1)
    grads.second(n - 1)
    for k in range(n):
        grads.third(k)
    acts.start()
    for k in range(n, 2 * n):
        grads.third(k)
    grads.sibling(0, 4 * n)

    every = range(shards)
    norms = {}

    def damp_grads():
        norms["grads"] = damp(cov, factor, damping_ref[1])

    def project(k):
        projected[k] = dot_nn(grad_low[...], grads_all[k]).astype(BF16)

    def lower():
        grad_low[...] = grad_work[...].astype(BF16)

    work = [
        functools.partial(cov_tile, grads_all, cov, every, i, j, False)
        for i in range(TILES)
        for j in range(i, TILES)
    ]
    work += [damp_grads]
    work += horner_steps(factor, grad_work, coeffs_ref, t * width, lambda: norms["grads"])
    work += [lower]
    work += [functools.partial(project, k) for k in every]
    relays = []
    for k in range(1, n):
        relays += [functools.partial(acts.line, k), functools.partial(acts.second, k - 1)]
    relays += [functools.partial(acts.second, n - 1)]
    relays += [functools.partial(acts.third, k) for k in range(n)]
    done = 0
    for index, chunk in enumerate(work):
        chunk()
        upto = (index + 1) * len(relays) // len(work)
        for relay in relays[done:upto]:
            relay()
        done = upto
    near = [2 * k + p.y for k in range(n)]
    far = [2 * k + 1 - p.y for k in range(n)]
    acts.sibling(0, 3 * n)
    tile = cov.shape[0] // TILES

    def right_rows(slabs, i, add):
        rows = pl.ds(i * tile, tile)
        low = jnp.concatenate([projected[k] for k in slabs], axis=1)
        product = dot_nt(lanes(acts_all, slabs, rows), low)
        right[rows, :] = right[rows, :] + product if add else product

    third = n
    for i in range(TILES):
        for j in range(i, TILES):
            cov_tile(acts_all, cov, near, i, j, False)
            if i + j > 0 and third < 2 * n:
                acts.third(third)
                third += 1
        right_rows(near, i, False)
    while third < 2 * n:
        acts.third(third)
        third += 1
    acts.sibling(3 * n, 4 * n)
    for i in range(TILES):
        for j in range(i, TILES):
            cov_tile(acts_all, cov, far, i, j, True)
    act_norm = damp(cov, factor, damping_ref[0])
    height = weight_ref.shape[0]
    for run in horner_steps(factor, act_work, coeffs_ref, s * height, lambda: act_norm):
        run()
    for i in range(TILES):
        right_rows(far, i, True)
    update = dot_nn(act_work[...], right[...], lax.Precision.HIGHEST)

    started = []

    def push(src, dst, pair, index, target):
        copy = pltpu.make_async_remote_copy(
            src_ref=src,
            dst_ref=dst,
            send_sem=pair[0].at[index],
            recv_sem=pair[1].at[index],
            device_id=target,
            device_id_type=MESH,
        )
        copy.start()
        started.append(copy)
        return copy

    shard_sums[s] = jnp.broadcast_to(total(update * update), shard_sums.shape[1:])
    copies = [
        push(shard_sums.at[s], shard_sums.at[s], pairs[8], k - 1, ((s + k) % shards, t))
        for k in range(1, shards)
    ]
    for copy in copies:
        copy.wait_recv()
    tensor_sums[t] = jnp.sum(shard_sums[...], axis=0)
    copies = [
        push(tensor_sums.at[t], tensor_sums.at[t], pairs[9], k - 1, (s, (t + k) % tensors))
        for k in range(1, tensors)
    ]
    for copy in copies:
        copy.wait_recv()
    square_sum = jnp.sum(tensor_sums[...], axis=0)[0:1, 0:1]
    d = cov.shape[0]
    mean_square = square_sum / (d * d)
    momentum = 0.9 * momentum_ref[...] + update / jnp.sqrt(mean_square + 1e-06)
    new_momentum_ref[...] = momentum
    new_weight = weight_ref[...].astype(F32) - 0.1 * momentum

    low = new_weight.astype(BF16)
    main = weight_all.shape[2]
    rest = width - main
    weight_all[s, :height, :] = low[:, :main]
    ones = eye(rest, rest, 0, 0).astype(F32).astype(BF16)
    weight_all[s, height:, :height] = dot_nt(ones, low[:, main:]).astype(BF16)

    def rows_of(z, y):
        return weight_all.at[z * Y_CHIPS + y]

    own = rows_of(p.z, p.y)
    across = (p.z * Y_CHIPS + 1 - p.y, t)
    lines = [
        push(own, own, pairs[10], k - 1, (((p.z + k) % n) * Y_CHIPS + p.y, t))
        for k in range(1, n)
    ]
    crossed = [push(own, own, pairs[11], 0, across)]
    for k in range(1, n):
        lines[k - 1].wait_recv()
        piece = rows_of(p.z_at(k), p.y)
        crossed.append(push(piece, piece, pairs[11], k, across))
    for copy in crossed:
        copy.wait_recv()
    rows = jnp.concatenate([weight_all[k, :height, :] for k in range(shards)], axis=0)
    ones = eye(main, main, 0, 0).astype(F32).astype(BF16)
    gathered_ref[:main, :] = dot_nt(ones, rows).astype(BF16)
    for k in range(shards):
        gathered_ref[main:, k * height : (k + 1) * height] = weight_all[k, height:, :height]
    for copy in started:
        copy.wait_send()
    grads.finish()
    acts.finish()


def on_device_whole(shards, tensors, acts, outgrads, weight, momentum, damping, coeffs):
    tokens, width = acts.shape
    height = weight.shape[0]
    d = width * tensors
    n = shards // Y_CHIPS
    vmem = pl.BlockSpec(memory_space=pltpu.VMEM)
    smem = pl.BlockSpec(memory_space=pltpu.SMEM)
    counts = [n - 1, n, 2 * n, 4 * n] * 2 + [shards - 1, tensors - 1, n - 1, n]
    sems = []
    for count in counts:
        sems += [pltpu.SemaphoreType.DMA((count,))] * 2
    new_momentum, gathered = pl.pallas_call(
        functools.partial(step_kernel, shards),
        out_shape=(
            jax.ShapeDtypeStruct((height, width), F32),
            jax.ShapeDtypeStruct((width, d), BF16),
        ),
        in_specs=[vmem, vmem, vmem, vmem, smem, smem],
        out_specs=(vmem, vmem),
        scratch_shapes=[
            pltpu.VMEM((shards, d, tokens), BF16),
            pltpu.VMEM((shards, d, tokens), BF16),
            pltpu.VMEM((d, d), F32),
            pltpu.VMEM((d, d), BF16),
            pltpu.VMEM((width, d), F32),
            pltpu.VMEM((width, d), BF16),
            pltpu.VMEM((height, d), F32),
            pltpu.VMEM((shards, width, tokens), BF16),
            pltpu.VMEM((d, width), F32),
            pltpu.VMEM((shards, height + width % 128, width // 128 * 128), BF16),
            pltpu.VMEM((shards, 8, 128), F32),
            pltpu.VMEM((tensors, 8, 128), F32),
        ]
        + sems,
        compiler_params=pltpu.CompilerParams(
            collective_id=0, has_side_effects=True, vmem_limit_bytes=56 * 2**20
        ),
    )(acts.T, outgrads.T, weight, momentum, damping, coeffs)
    return new_momentum, gathered.T


def solution(mesh):
    in_specs = (
        P("shard", "tensor"),
        P("shard", "tensor"),
        P("shard", "tensor"),
        P("shard", "tensor"),
        P(),
        P(),
    )
    out_specs = (P("shard", "tensor"), P(None, "tensor"))
    shards, tensors = mesh.shape["shard"], mesh.shape["tensor"]

    def local(acts, *rest):
        held = 2 * acts.dtype.itemsize * acts.size * shards * tensors
        if held <= 24 * 2**20:
            return on_device_whole(shards, tensors, acts, *rest)
        return on_device(acts, *rest)

    return jax.shard_map(
        local, mesh=mesh, in_specs=in_specs, out_specs=out_specs, check_vma=False
    )
```
